32 devices in a mesh: plant: 8 (over z, core), col: 4 (over y, x).
Axes of the slice: x: 2, y: 2, z: 4, core: 2. Of those that a mesh axis runs over, the one named last changes fastest.
Arguments:
- tiles: bfloat16 [8, 4, 48, 256, 256], P('plant', 'col'), may hold values from -0.109375 to 0.109375
- tile_row: int32 [8, 4, 48], P('plant', 'col'), may hold values from 0 to 15
- tile_col: int32 [8, 4, 48], P('plant', 'col'), may hold values from 0 to 63
- row_count: int32 [8], P('plant'), may hold values from 2048 to 4096, as said below
- x_start: float32 [32, 65536], P(None, 'col'), may hold values from 0 to 1
- y_start: float32 [32, 32768], P(None, 'plant'), may hold values from 0 to 1
- cost: float32 [65536], P('col'), may hold values from -3 to 3
- upper: float32 [65536], P('col'), may hold values from 0.5 to 2
- demand: float32 [32, 32768], P(None, 'plant'), may hold values from -6 to 6
- tau: float32 [32], replicated, may hold values from 0.2 to 1
- sigma: float32 [32], replicated, may hold values from 0.2 to 1
Outputs:
- primal: float32 [32, 65536], P(None, 'col')
- dual: float32 [32, 32768], P(None, 'plant')
The draws below stay inside these ranges and needn't reach their ends.
Inputs may be any that keep to these rules, and one draw needn't show every extreme that they name: Each plant block has row_count live rows, the first ones of its block; at least one plant block is full. `tile_row`: tiles at the same position add up.
All inputs are finite; a program needn't handle non-finite values.
Results may differ from the reference program's by a relative error of at most 0.003.
Values sent between devices are 32-bit elements; how exact they have to be, the bound alone decides.
No kernel may reach another device: no remote copies, remote signals or barrier semaphores. Data moves between devices by JAX's collectives and lax.ppermute only.
A program may use at most 64 MiB of HBM per device.

```python
import math
import jax
import jax.numpy as jnp
from jax import lax

SCEN = 32
TILE = 256
COLT_DEV = 64
ROWT_DEV = 16
TILES_DEV = 48
ITERS = 3
ROWS_DEV = 4096
NROWS = 32768
NVAR = 65536
N_PLANT = 8
N_COL = 4


def draw_row_count(key, part):
    first = jax.random.fold_in(key, 11)
    second = jax.random.fold_in(key, 12)
    counts = jax.random.randint(first, (N_PLANT,), ROWS_DEV // 2, ROWS_DEV + 1)
    chosen = jax.random.randint(second, (), 0, N_PLANT)
    return jnp.where(jnp.arange(N_PLANT) == chosen, ROWS_DEV, counts).astype(jnp.int32)


def place_ends(drawn, rng, low, largest):
    index_at = [jax.random.randint(jax.random.fold_in(rng, axis), (), 0, length) for axis, length in enumerate(drawn.shape)]
    longest = drawn.shape.index(max(drawn.shape))
    next_to = index_at[:longest] + [(index_at[longest] + 1) % drawn.shape[longest]] + index_at[longest + 1:]
    return drawn.at[tuple(index_at)].set(low).at[tuple(next_to)].set(largest)


def shard_levels(rng, shape, pieces, smallest, high):
    loudness = 1.0
    for axis_at, shards_of in pieces:
        steps = jax.random.uniform(jax.random.fold_in(jax.random.fold_in(rng, 6), axis_at), (shards_of,), jnp.float32, smallest / len(pieces), high / len(pieces))
        loudness = loudness * jnp.repeat(jnp.exp(steps), shape[axis_at] // shards_of).reshape((-1,) + (1,) * (len(shape) - 1 - axis_at))
    return loudness


def centred(own_key, extent, width, most, pieces=(), kind=jnp.bfloat16):
    gain = shard_levels(own_key, extent, pieces, -0.22, 0.18) if pieces else 1.0
    array = jax.random.normal(own_key, extent, jnp.float32) * width * gain
    return jnp.minimum(jnp.maximum(array, -most), most).astype(kind)


def setup_inputs(seed: int = 0) -> dict:
    streams_of = jax.random.split(jax.random.key(seed), 12)
    tiles = centred(streams_of[0], (N_PLANT, N_COL, TILES_DEV, TILE, TILE), (TILE * TILES_DEV * N_COL // ROWT_DEV) ** -0.5, 0.109375, ((0, 8), (1, 4)))
    tile_row = place_ends(jax.random.randint(streams_of[1], (N_PLANT, N_COL, TILES_DEV), 0, ROWT_DEV), jax.random.fold_in(streams_of[1], 1), 0, ROWT_DEV - 1).astype(jnp.int32)
    tile_col = place_ends(jax.random.randint(streams_of[2], (N_PLANT, N_COL, TILES_DEV), 0, COLT_DEV), jax.random.fold_in(streams_of[2], 1), 0, COLT_DEV - 1).astype(jnp.int32)
    row_count = draw_row_count(jax.random.fold_in(streams_of[11], 71), 0)
    x_start = jnp.clip(1.0 * jax.random.uniform(streams_of[4], (SCEN, NVAR), jnp.float32) ** shard_levels(streams_of[4], (SCEN, NVAR), ((1, 4),), -0.2, 0.2), 0.0, 1.0)
    y_start = jnp.clip(1.0 * jax.random.uniform(streams_of[5], (SCEN, NROWS), jnp.float32) ** shard_levels(streams_of[5], (SCEN, NROWS), ((1, 8),), -0.2, 0.2), 0.0, 1.0)
    cost = centred(streams_of[6], (NVAR,), 0.5, 3.0, ((0, 4),), jnp.float32)
    upper = jnp.clip(0.5 + 1.5 * jax.random.uniform(streams_of[7], (NVAR,), jnp.float32) ** shard_levels(streams_of[7], (NVAR,), ((0, 4),), -0.2, 0.2), 0.5, 2.0)
    demand = centred(streams_of[8], (SCEN, NROWS), 1.0, 6.0, ((1, 8),), jnp.float32)
    tau = jnp.clip(jnp.exp(jax.random.uniform(streams_of[9], (SCEN,), jnp.float32, math.log(0.2), math.log(1.0))), 0.2, 1.0)
    sigma = jnp.clip(jnp.exp(jax.random.uniform(streams_of[10], (SCEN,), jnp.float32, math.log(0.2), math.log(1.0))), 0.2, 1.0)
    return dict(tiles=tiles, tile_row=tile_row, tile_col=tile_col, row_count=row_count, x_start=x_start, y_start=y_start, cost=cost, upper=upper, demand=demand, tau=tau, sigma=sigma)


def transpose_block(dual_part, blocks, rows, cols):
    picked = jnp.take(dual_part, rows, axis=1).astype(jnp.float32)
    contrib = jnp.einsum("str,trc->stc", picked, blocks.astype(jnp.float32), precision=lax.Precision.HIGHEST)
    col_hot = (jnp.arange(COLT_DEV, dtype=jnp.int32)[:, None] == cols[None, :]).astype(jnp.float32)
    return jnp.einsum("kt,stc->skc", col_hot, contrib, precision=lax.Precision.HIGHEST)


def forward_block(primal_part, blocks, rows, cols):
    picked = jnp.take(primal_part, cols, axis=1).astype(jnp.float32)
    contrib = jnp.einsum("stc,trc->str", picked, blocks.astype(jnp.float32), precision=lax.Precision.HIGHEST)
    row_hot = (jnp.arange(ROWT_DEV, dtype=jnp.int32)[:, None] == rows[None, :]).astype(jnp.float32)
    return jnp.einsum("kt,str->skr", row_hot, contrib, precision=lax.Precision.HIGHEST)


def reference(tiles, tile_row, tile_col, row_count, x_start, y_start, cost, upper, demand, tau, sigma):
    n_plant = tiles.shape[0]
    n_col = tiles.shape[1]
    rows_dev = ROWT_DEV * TILE
    live = (jnp.arange(rows_dev, dtype=jnp.int32)[None, :] < row_count[:, None]).astype(jnp.float32).reshape(-1)
    primal = x_start
    dual = y_start * live[None, :]
    for iteration in range(ITERS):
        dual_low = dual.astype(jnp.bfloat16).reshape(SCEN, n_plant, ROWT_DEV, TILE)

        def column_shard(shard):
            def accumulate(total, plant_index):
                term = transpose_block(dual_low[:, plant_index], tiles[plant_index, shard], tile_row[plant_index, shard], tile_col[plant_index, shard])
                return total + term, None
            start = jnp.zeros((SCEN, COLT_DEV, TILE), jnp.float32)
            total, unused = lax.scan(accumulate, start, jnp.arange(n_plant, dtype=jnp.int32))
            return total

        kty = lax.map(column_shard, jnp.arange(n_col, dtype=jnp.int32))
        kty = jnp.transpose(kty, (1, 0, 2, 3)).reshape(SCEN, -1)
        primal_new = jnp.minimum(jnp.maximum(primal - tau[:, None] * (cost[None, :] - kty), 0.0), upper[None, :])
        extra = (2.0 * primal_new - primal).astype(jnp.bfloat16).reshape(SCEN, n_col, COLT_DEV, TILE)

        def plant_block(plant_index):
            def accumulate(total, shard):
                term = forward_block(extra[:, shard], tiles[plant_index, shard], tile_row[plant_index, shard], tile_col[plant_index, shard])
                return total + term, None
            start = jnp.zeros((SCEN, ROWT_DEV, TILE), jnp.float32)
            total, unused = lax.scan(accumulate, start, jnp.arange(n_col, dtype=jnp.int32))
            return total

        kx = lax.map(plant_block, jnp.arange(n_plant, dtype=jnp.int32))
        kx = jnp.transpose(kx, (1, 0, 2, 3)).reshape(SCEN, -1)
        dual = jnp.maximum(dual + sigma[:, None] * (demand - kx), 0.0) * live[None, :]
        primal = primal_new
    return primal, dual
```

```python
import functools

import jax
import jax.numpy as jnp
from jax import lax
from jax.experimental import pallas as pl
from jax.experimental.pallas import tpu as pltpu
from jax.sharding import PartitionSpec as P

ITERS = 3
GROUPS = 2
VMEM_LIMIT = 40 << 20


def vmem():
    return pl.BlockSpec(memory_space=pltpu.VMEM)


def smem():
    return pl.BlockSpec(memory_space=pltpu.SMEM)


def row_block(rows, width, group):
    return pl.BlockSpec((rows, width), lambda i: (group, 0))


def whole(shape):
    return pl.BlockSpec(shape, lambda i: (0,) * len(shape))


def scalars():
    return pl.BlockSpec(memory_space=pltpu.SMEM)


def dual_kernel(first, n_tiles, tile_rows, tile_cols, width, *refs):
    if first:
        (rows_ref, cols_ref, info_ref, tiles_ref, y_ref,
         dual_ref, q0, q1, q2, q3, low, prods, acc) = refs
    else:
        (rows_ref, cols_ref, info_ref, tiles_ref, y_ref, demand_ref, sigma_ref,
         l_ref, l2_ref, r_ref, r2_ref,
         dual_ref, q0, q1, q2, q3, low, prods, acc) = refs
    scen = y_ref.shape[0]
    count, core, parity = info_ref[0], info_ref[1], info_ref[2]
    lane = lax.broadcasted_iota(jnp.int32, (scen, width), 1)
    half = tile_rows // 2
    if not first:
        sigma = jnp.broadcast_to(sigma_ref[...], (scen, width))
    for j in range(tile_rows):
        at = pl.ds(j * width, width)
        live = (lane < count - j * width).astype(jnp.float32)
        if first:
            dual = y_ref[:, at] * live
        else:
            if j < half:
                kx = l_ref[j] + l2_ref[j]
            else:
                kx = r_ref[j - half] + r2_ref[j - half]
            dual = jnp.maximum(y_ref[:, at] + sigma * (demand_ref[:, at] - kx), 0.0) * live
        dual_ref[:, at] = dual
        low[j] = dual.astype(jnp.bfloat16)
    for t in range(n_tiles):
        prods[t] = jnp.dot(low[rows_ref[t]], tiles_ref[t], preferred_element_type=jnp.float32)
    acc[...] = jnp.zeros(acc.shape, jnp.float32)
    quarter = tile_cols // 4
    for t in range(n_tiles):
        col = cols_ref[t]
        part = col // quarter
        slot = (part ^ (core * 2 + parity)) * quarter + col % quarter
        acc[slot] += prods[t]
    for i, ref in enumerate((q0, q1, q2, q3)):
        ref[...] = acc[pl.ds(i * quarter, quarter)]


def last_dual_kernel(tile_rows, width, info_ref, y_ref, demand_ref, sigma_ref, l_ref, l2_ref, r_ref, r2_ref, *rest):
    dual_ref = rest[-1]
    scen = y_ref.shape[0]
    count = info_ref[0]
    lane = lax.broadcasted_iota(jnp.int32, (scen, width), 1)
    half = tile_rows // 2
    sigma = jnp.broadcast_to(sigma_ref[...], (scen, width))
    for j in range(tile_rows):
        at = pl.ds(j * width, width)
        live = (lane < count - j * width).astype(jnp.float32)
        if j < half:
            kx = l_ref[j] + l2_ref[j]
        else:
            kx = r_ref[j - half] + r2_ref[j - half]
        dual_ref[:, at] = jnp.maximum(y_ref[:, at] + sigma * (demand_ref[:, at] - kx), 0.0) * live


def primal_kernel(n_tiles, tile_rows, tile_cols, width, has_into, *refs):
    (rows_ref, cols_ref, info_ref, tiles_ref, x_ref, cost_ref, upper_ref, tau_ref,
     k0, k1, k2, k3) = refs[:12]
    refs = refs[12 + has_into:]
    primal_ref, l_ref, r_ref, extra, prods, acc = refs
    scen = x_ref.shape[0]
    core, parity = info_ref[1], info_ref[2]
    quarter = tile_cols // 4
    half = tile_rows // 2
    tau = jnp.broadcast_to(tau_ref[...], (scen, width))
    for i, ref in enumerate((k0, k1, k2, k3)):
        base = ((core * 2 + parity) ^ i) * quarter
        for j in range(quarter):
            at = pl.ds(pl.multiple_of((base + j) * width, width), width)
            old = x_ref[:, at]
            new = jnp.minimum(
                jnp.maximum(old - tau * (cost_ref[:, at] - ref[j]), 0.0), upper_ref[:, at]
            )
            primal_ref[:, at] = new
            extra[base + j] = (2.0 * new - old).astype(jnp.bfloat16)
    for t in range(n_tiles):
        prods[t] = lax.dot_general(
            extra[cols_ref[t]], tiles_ref[t], (((1,), (1,)), ((), ())),
            preferred_element_type=jnp.float32,
        )
    acc[...] = jnp.zeros(acc.shape, jnp.float32)
    for t in range(n_tiles):
        acc[rows_ref[t]] += prods[t]
    l_ref[...] = acc[pl.ds(0, half)]
    r_ref[...] = acc[pl.ds(half, half)]


def body(tiles, tile_row, tile_col, row_count, x_start, y_start, cost, upper, demand, tau, sigma,
         *, n_plant, n_col):
    f32 = jnp.float32
    blocks = tiles[0, 0]
    rows = tile_row[0, 0]
    cols = tile_col[0, 0]
    n_tiles, width, _ = blocks.shape
    scenarios, rows_dev = y_start.shape
    col_width = x_start.shape[1]
    tile_rows = rows_dev // width
    tile_cols = col_width // width
    quarter = tile_cols // 4
    half = tile_rows // 2
    m = scenarios // GROUPS
    plant = lax.axis_index("plant")
    info = jnp.stack([row_count[0], plant & 1, (plant >> 1) & 1]).astype(jnp.int32)
    cost_row = cost[None, :]
    upper_row = upper[None, :]
    tau_col = tau[:, None]
    sigma_col = sigma[:, None]
    params = pltpu.CompilerParams(vmem_limit_bytes=VMEM_LIMIT)
    quarters = [jax.ShapeDtypeStruct((quarter, m, width), f32)] * 4
    halves = [jax.ShapeDtypeStruct((half, m, width), f32)] * 2
    flops = 2 * n_tiles * m * width * width
    estimate = pl.CostEstimate(flops=flops, bytes_accessed=n_tiles * width * width * 2, transcendentals=0)

    def swap(value, axis, size, bit):
        return lax.ppermute(value, axis, [(i, i ^ bit) for i in range(size)])

    def y_spec(arr, group):
        return row_block(m, rows_dev, group if arr.shape[0] == scenarios else 0)

    def x_spec(arr, group):
        return row_block(m, col_width, group if arr.shape[0] == scenarios else 0)

    def step_dual(group, dual, parts):
        first = parts is None
        args = [rows, cols, info, blocks, dual]
        specs = [scalars(), scalars(), scalars(), whole(blocks.shape), y_spec(dual, group)]
        if not first:
            args += [demand, sigma_col, *parts]
            specs += [y_spec(demand, group), row_block(m, 1, group)] + [whole((half, m, width))] * 4
        return pl.pallas_call(
            functools.partial(dual_kernel, first, n_tiles, tile_rows, tile_cols, width),
            grid=(1,),
            in_specs=specs,
            out_shape=[jax.ShapeDtypeStruct((m, rows_dev), f32)] + quarters,
            out_specs=[whole((m, rows_dev))] + [whole((quarter, m, width))] * 4,
            scratch_shapes=[
                pltpu.VMEM((tile_rows, m, width), jnp.bfloat16),
                pltpu.VMEM((n_tiles, m, width), f32),
                pltpu.VMEM((tile_cols, m, width), f32),
            ],
            compiler_params=params,
            cost_estimate=estimate,
            name="dual_step",
        )(*args)

    def step_primal(group, primal, kty, into, last):
        args = [rows, cols, info, blocks, primal, cost_row, upper_row, tau_col, *kty]
        specs = [scalars(), scalars(), scalars(), whole(blocks.shape), x_spec(primal, group),
                 whole((1, col_width)), whole((1, col_width)), row_block(m, 1, group)]
        specs += [whole((quarter, m, width))] * 4
        aliases = {}
        if into is not None:
            aliases = {len(args): 0}
            args.append(into)
            specs.append(pl.BlockSpec(memory_space=pl.ANY))
        out = jax.ShapeDtypeStruct((scenarios if last else m, col_width), f32)
        return pl.pallas_call(
            functools.partial(primal_kernel, n_tiles, tile_rows, tile_cols, width, int(into is not None)),
            grid=(1,),
            in_specs=specs,
            out_shape=[out] + halves,
            out_specs=[row_block(m, col_width, group if last else 0)] + [whole((half, m, width))] * 2,
            scratch_shapes=[
                pltpu.VMEM((tile_cols, m, width), jnp.bfloat16),
                pltpu.VMEM((n_tiles, m, width), f32),
                pltpu.VMEM((tile_rows, m, width), f32),
            ],
            input_output_aliases=aliases,
            compiler_params=params,
            cost_estimate=estimate,
            name="primal_step",
        )(*args)

    def finish_dual(group, dual, parts, into):
        args = [info, dual, demand, sigma_col, *parts]
        specs = [scalars(), y_spec(dual, group), y_spec(demand, group), row_block(m, 1, group)]
        specs += [whole((half, m, width))] * 4
        aliases = {}
        if into is not None:
            aliases = {len(args): 0}
            args.append(into)
            specs.append(pl.BlockSpec(memory_space=pl.ANY))
        return pl.pallas_call(
            functools.partial(last_dual_kernel, tile_rows, width),
            grid=(1,),
            in_specs=specs,
            out_shape=jax.ShapeDtypeStruct((scenarios, rows_dev), f32),
            out_specs=row_block(m, rows_dev, group),
            input_output_aliases=aliases,
            compiler_params=params,
            name="dual_end",
        )(*args)

    def over_plant(q0, q1, q2, q3):
        g1 = swap(q3, "plant", n_plant, 1)
        g0 = swap(q2, "plant", n_plant, 1)
        own = q0 + g0 + swap(q1 + g1, "plant", n_plant, 2)
        bit = 4
        while bit < n_plant:
            own = own + swap(own, "plant", n_plant, bit)
            bit *= 2
        pair = swap(own, "plant", n_plant, 2)
        return own, pair, swap(own, "plant", n_plant, 1), swap(pair, "plant", n_plant, 1)

    def over_col(l, r):
        bits = []
        bit = 1
        while bit < n_col:
            bits.append(bit)
            bit *= 2
        turned = bits[len(bits) // 2:] + bits[:len(bits) // 2]
        for a, b in zip(bits[:-1], turned[:-1]):
            l, r = l + swap(l, "col", n_col, a), r + swap(r, "col", n_col, b)
        return l, swap(l, "col", n_col, bits[-1]), r, swap(r, "col", n_col, turned[-1])

    duals = [y_start] * GROUPS
    primals = [x_start] * GROUPS
    parts = [None] * GROUPS
    primal_out = None
    for iteration in range(ITERS):
        last = iteration == ITERS - 1
        for g in range(GROUPS):
            duals[g], *qs = step_dual(g, duals[g], parts[g])
            kty = over_plant(*qs)
            primals[g], l, r = step_primal(g, primals[g], kty, primal_out if last else None, last)
            if last:
                primal_out = primals[g]
            parts[g] = over_col(l, r)
    dual_out = None
    for g in range(GROUPS):
        dual_out = finish_dual(g, duals[g], parts[g], dual_out)
    return primal_out, dual_out


def solution(mesh):
    placed = (
        P("plant", "col", None, None, None),
        P("plant", "col", None),
        P("plant", "col", None),
        P("plant"),
        P(None, "col"),
        P(None, "plant"),
        P("col"),
        P("col"),
        P(None, "plant"),
        P(),
        P(),
    )
    return jax.shard_map(
        functools.partial(body, n_plant=mesh.shape["plant"], n_col=mesh.shape["col"]),
        mesh=mesh,
        in_specs=placed,
        out_specs=(P(None, "col"), P(None, "plant")),
        check_vma=False,
    )
```

```python
import functools

import jax
import jax.numpy as jnp
from jax import lax
from jax.experimental import pallas as pl
from jax.experimental.pallas import tpu as pltpu
from jax.sharding import PartitionSpec as P

ITERS = 3
GROUPS = 2
VMEM_LIMIT = 24 << 20
LAG = 10.0
TIE = True


def row_block(rows, width, group):
    return pl.BlockSpec((rows, width), lambda i: (group, 0))


def whole(shape):
    return pl.BlockSpec(shape, lambda i: (0,) * len(shape))


def scalars():
    return pl.BlockSpec(memory_space=pltpu.SMEM)


def dual_kernel(first, n_tiles, tile_rows, tile_cols, width, *refs):
    if first:
        (meta_ref, tiles_ref, y_ref,
         dual_ref, q0, q1, q2, q3, low, prods, acc) = refs
    else:
        (meta_ref, tiles_ref, y_ref, demand_ref, sigma_ref,
         l_ref, l2_ref, r_ref, r2_ref,
         dual_ref, q0, q1, q2, q3, low, prods, acc) = refs
    scen = y_ref.shape[0]
    count = meta_ref[3, 0]
    lane = lax.broadcasted_iota(jnp.int32, (scen, width), 1)
    half = tile_rows // 2
    if not first:
        sigma = sigma_ref[...]
    for j in range(tile_rows):
        at = pl.ds(j * width, width)
        live = (lane < count - j * width).astype(jnp.float32)
        if first:
            dual = y_ref[:, at] * live
        else:
            if j < half:
                kx = l_ref[j] + l2_ref[j]
            else:
                kx = r_ref[j - half] + r2_ref[j - half]
            dual = jnp.maximum(y_ref[:, at] + sigma * (demand_ref[:, at] - kx), 0.0) * live
        dual_ref[:, at] = dual
        low[j] = dual.astype(jnp.bfloat16)
    for t in range(n_tiles):
        prods[t] = jnp.dot(low[meta_ref[0, t]], tiles_ref[t], preferred_element_type=jnp.float32)
    acc[...] = jnp.zeros(acc.shape, jnp.float32)
    quarter = tile_cols // 4
    for t in range(n_tiles):
        acc[meta_ref[2, t]] += prods[t]
    for i, ref in enumerate((q0, q1, q2, q3)):
        ref[...] = acc[pl.ds(i * quarter, quarter)]


def last_dual_kernel(tile_rows, width, meta_ref, y_ref, demand_ref, sigma_ref, l_ref, l2_ref, r_ref, r2_ref, *rest):
    dual_ref = rest[-1]
    scen = y_ref.shape[0]
    count = meta_ref[3, 0]
    lane = lax.broadcasted_iota(jnp.int32, (scen, width), 1)
    half = tile_rows // 2
    sigma = sigma_ref[...]
    for j in range(tile_rows):
        at = pl.ds(j * width, width)
        live = (lane < count - j * width).astype(jnp.float32)
        if j < half:
            kx = l_ref[j] + l2_ref[j]
        else:
            kx = r_ref[j - half] + r2_ref[j - half]
        dual_ref[:, at] = jnp.maximum(y_ref[:, at] + sigma * (demand_ref[:, at] - kx), 0.0) * live


def primal_kernel(n_tiles, tile_rows, tile_cols, width, has_into, *refs):
    (meta_ref, tiles_ref, x_ref, cost_ref, upper_ref, tau_ref,
     k0, k1, k2, k3) = refs[:10]
    refs = refs[10 + has_into:]
    primal_ref, l_ref, r_ref, extra, prods, acc = refs
    scen = x_ref.shape[0]
    place = meta_ref[3, 1]
    quarter = tile_cols // 4
    half = tile_rows // 2
    tau = tau_ref[...]
    for i, ref in enumerate((k0, k1, k2, k3)):
        base = (place ^ i) * quarter
        for j in range(quarter):
            at = pl.ds(pl.multiple_of((base + j) * width, width), width)
            old = x_ref[:, at]
            new = jnp.minimum(
                jnp.maximum(old - tau * (cost_ref[:, at] - ref[j]), 0.0), upper_ref[:, at]
            )
            primal_ref[:, at] = new
            extra[base + j] = (2.0 * new - old).astype(jnp.bfloat16)
    for t in range(n_tiles):
        prods[t] = lax.dot_general(
            extra[meta_ref[1, t]], tiles_ref[t], (((1,), (1,)), ((), ())),
            preferred_element_type=jnp.float32,
        )
    acc[...] = jnp.zeros(acc.shape, jnp.float32)
    for t in range(n_tiles):
        acc[meta_ref[0, t]] += prods[t]
    l_ref[...] = acc[pl.ds(0, half)]
    r_ref[...] = acc[pl.ds(half, half)]


def body(tiles, tile_row, tile_col, row_count, x_start, y_start, cost, upper, demand, tau, sigma,
         *, n_plant, n_col):
    f32 = jnp.float32
    blocks = tiles[0, 0]
    rows = tile_row[0, 0]
    cols = tile_col[0, 0]
    n_tiles, width, _ = blocks.shape
    scenarios, rows_dev = y_start.shape
    col_width = x_start.shape[1]
    tile_rows = rows_dev // width
    tile_cols = col_width // width
    quarter = tile_cols // 4
    half = tile_rows // 2
    m = scenarios // GROUPS
    plant = lax.axis_index("plant")
    place = (plant & 1) * 2 + (plant >> 1) % 2
    slots = ((cols // quarter) ^ place) * quarter + cols % quarter
    lane = lax.iota(jnp.int32, n_tiles)
    info = jnp.where(lane == 0, row_count[0], place)
    meta = jnp.stack([rows, cols, slots, info]).astype(jnp.int32)
    cost_row = cost[None, :]
    upper_row = upper[None, :]
    tau_col = jnp.broadcast_to(tau[:, None], (scenarios, width))
    sigma_col = jnp.broadcast_to(sigma[:, None], (scenarios, width))
    params = pltpu.CompilerParams(vmem_limit_bytes=VMEM_LIMIT)
    quarters = [jax.ShapeDtypeStruct((quarter, m, width), f32)] * 4
    halves = [jax.ShapeDtypeStruct((half, m, width), f32)] * 2
    flops = 2 * n_tiles * m * width * width
    estimate = pl.CostEstimate(flops=10**11, bytes_accessed=10**9, transcendentals=0)

    def swap(value, axis, size, bit):
        return lax.ppermute(value, axis, [(i, i ^ bit) for i in range(size)])

    def y_spec(arr, group):
        return row_block(m, rows_dev, group if arr.shape[0] == scenarios else 0)

    def x_spec(arr, group):
        return row_block(m, col_width, group if arr.shape[0] == scenarios else 0)

    def step_dual(group, dual, parts):
        first = parts is None
        args = [meta, blocks, dual]
        specs = [scalars(), whole(blocks.shape), y_spec(dual, group)]
        if not first:
            args += [demand, sigma_col, *parts]
            specs += [y_spec(demand, group), row_block(m, width, group)] + [whole((half, m, width))] * 4
        return pl.pallas_call(
            functools.partial(dual_kernel, first, n_tiles, tile_rows, tile_cols, width),
            grid=(1,),
            in_specs=specs,
            out_shape=[jax.ShapeDtypeStruct((m, rows_dev), f32)] + quarters,
            out_specs=[whole((m, rows_dev))] + [whole((quarter, m, width))] * 4,
            scratch_shapes=[
                pltpu.VMEM((tile_rows, m, width), jnp.bfloat16),
                pltpu.VMEM((n_tiles, m, width), f32),
                pltpu.VMEM((tile_cols, m, width), f32),
            ],
            compiler_params=params,
            cost_estimate=estimate,
            name="dual_step",
        )(*args)

    def step_primal(group, primal, kty, into, last):
        args = [meta, blocks, primal, cost_row, upper_row, tau_col, *kty]
        specs = [scalars(), whole(blocks.shape), x_spec(primal, group),
                 whole((1, col_width)), whole((1, col_width)), row_block(m, width, group)]
        specs += [whole((quarter, m, width))] * 4
        aliases = {}
        if into is not None:
            aliases = {len(args): 0}
            args.append(into)
            specs.append(pl.BlockSpec(memory_space=pl.ANY))
        out = jax.ShapeDtypeStruct((scenarios if last else m, col_width), f32)
        return pl.pallas_call(
            functools.partial(primal_kernel, n_tiles, tile_rows, tile_cols, width, int(into is not None)),
            grid=(1,),
            in_specs=specs,
            out_shape=[out] + halves,
            out_specs=[row_block(m, col_width, group if last else 0)] + [whole((half, m, width))] * 2,
            scratch_shapes=[
                pltpu.VMEM((tile_cols, m, width), jnp.bfloat16),
                pltpu.VMEM((n_tiles, m, width), f32),
                pltpu.VMEM((tile_rows, m, width), f32),
            ],
            input_output_aliases=aliases,
            compiler_params=params,
            cost_estimate=estimate,
            name="primal_step",
        )(*args)

    def finish_dual(group, dual, parts, into):
        args = [meta, dual, demand, sigma_col, *parts]
        specs = [scalars(), y_spec(dual, group), y_spec(demand, group), row_block(m, width, group)]
        specs += [whole((half, m, width))] * 4
        aliases = {}
        if into is not None:
            aliases = {len(args): 0}
            args.append(into)
            specs.append(pl.BlockSpec(memory_space=pl.ANY))
        return pl.pallas_call(
            functools.partial(last_dual_kernel, tile_rows, width),
            grid=(1,),
            in_specs=specs,
            out_shape=jax.ShapeDtypeStruct((scenarios, rows_dev), f32),
            out_specs=row_block(m, rows_dev, group),
            input_output_aliases=aliases,
            compiler_params=params,
            name="dual_end",
        )(*args)

    final = {"primal": None, "dual": None}

    def run(group):
        dual, primal, parts = y_start, x_start, None
        for iteration in range(ITERS):
            last = iteration == ITERS - 1
            dual, q0, q1, q2, q3 = step_dual(group, dual, parts)
            g1 = swap(q3, "plant", n_plant, 1)
            g0 = swap(q2, "plant", n_plant, 1)
            q1, g1 = yield q1, g1
            q1 = swap(q1 + g1, "plant", n_plant, 2)
            q0, g0, q1 = yield q0, g0, q1
            own = q0 + g0 + q1
            bit = 4
            while bit < n_plant:
                near = swap(own, "plant", n_plant, bit)
                bit *= 2
                own, near = yield own, near
                own = own + near
            pair = swap(own, "plant", n_plant, 2)
            other = swap(own, "plant", n_plant, 1)
            own, pair = yield own, pair
            across = swap(pair, "plant", n_plant, 1)
            own, pair, other, across = yield own, pair, other, across
            kty = (own, pair, other, across)
            into = final["primal"] if last else None
            primal, l, r = step_primal(group, primal, kty, into, last)
            if last:
                final["primal"] = primal
            for a, b in zip(bits, turned):
                l2, r2 = swap(l, "col", n_col, a), swap(r, "col", n_col, b)
                l, l2, r, r2 = yield l, l2, r, r2
                if a != bits[-1]:
                    l, r = l + l2, r + r2
            parts = (l, l2, r, r2)
        final["dual"] = finish_dual(group, dual, parts, final["dual"])

    bits = []
    bit = 1
    while bit < n_col:
        bits.append(bit)
        bit *= 2
    turned = bits[len(bits) // 2:] + bits[:len(bits) // 2]
    runs = [run(g) for g in range(GROUPS)]
    held = [next(r) for r in runs]
    token = None
    for g in order(GROUPS, n_plant, n_col):
        values = held[g]
        if TIE:
            if token is not None:
                *values, token = lax.optimization_barrier((*values, token))
            else:
                token = values[0]
                values = list(values)
        try:
            held[g] = runs[g].send(tuple(values))
            if TIE:
                token, _ = lax.optimization_barrier((token, held[g][0]))
        except StopIteration:
            pass
    return final["primal"], final["dual"]


def order(groups, n_plant, n_col):
    mids = max(n_plant.bit_length() - 3, 0)
    lengths = [4.0, 9.5] + [15.0] * mids + [8.0, 2.0] + [8.0] * (n_col.bit_length() - 1)
    events = []
    for g in range(groups):
        at = LAG * g
        for i in range(ITERS):
            for j, length in enumerate(lengths):
                at += length
                events.append((at, g))
    return [g for _, g in sorted(events)]


def solution(mesh):
    placed = (
        P("plant", "col", None, None, None),
        P("plant", "col", None),
        P("plant", "col", None),
        P("plant"),
        P(None, "col"),
        P(None, "plant"),
        P("col"),
        P("col"),
        P(None, "plant"),
        P(),
        P(),
    )
    return jax.shard_map(
        functools.partial(body, n_plant=mesh.shape["plant"], n_col=mesh.shape["col"]),
        mesh=mesh,
        in_specs=placed,
        out_specs=(P(None, "col"), P(None, "plant")),
        check_vma=False,
    )
```

```python
import functools

import jax
import jax.numpy as jnp
from jax import lax
from jax.experimental import pallas as pl
from jax.experimental.pallas import tpu as pltpu
from jax.sharding import PartitionSpec as P

ITERS = 3
GROUPS = 2
VMEM_LIMIT = 24 << 20
LAG = 19.4
STEPS = [4.0, 11.1, 15.0, 8.9, 2.0, 8.0, 8.4]
DUAL_COST = 10**11
PRIMAL_COST = 10**11
TIE = True


def row_block(rows, width, group):
    return pl.BlockSpec((rows, width), lambda i: (group, 0))


def whole(shape):
    return pl.BlockSpec(shape, lambda i: (0,) * len(shape))


def scalars():
    return pl.BlockSpec(memory_space=pltpu.SMEM)


def spread(col, place, quarter):
    if quarter & (quarter - 1):
        part = lax.div(col, quarter)
        return (part ^ place) * quarter + (col - part * quarter)
    return col ^ (place * quarter)


def dual_kernel(first, n_tiles, tile_rows, tile_cols, width, *refs):
    if first:
        (meta_ref, tiles_ref, y_ref,
         dual_ref, q0, q1, q2, q3, low, prods, acc) = refs
    else:
        (meta_ref, tiles_ref, y_ref, demand_ref, sigma_ref,
         l_ref, l2_ref, r_ref, r2_ref,
         dual_ref, q0, q1, q2, q3, low, prods, acc) = refs
    scen = y_ref.shape[0]
    count, place = meta_ref[2, 0], meta_ref[2, 1]
    lane = lax.broadcasted_iota(jnp.int32, (scen, width), 1)
    half = tile_rows // 2
    if not first:
        sigma = sigma_ref[...]
    for j in range(tile_rows):
        at = pl.ds(j * width, width)
        live = (lane < count - j * width).astype(jnp.float32)
        if first:
            dual = y_ref[:, at] * live
        else:
            if j < half:
                kx = l_ref[j] + l2_ref[j]
            else:
                kx = r_ref[j - half] + r2_ref[j - half]
            dual = jnp.maximum(y_ref[:, at] + sigma * (demand_ref[:, at] - kx), 0.0) * live
        dual_ref[:, at] = dual
        low[j] = dual.astype(jnp.bfloat16)
    for t in range(n_tiles):
        prods[t] = jnp.dot(low[meta_ref[0, t]], tiles_ref[t], preferred_element_type=jnp.float32)
    acc[...] = jnp.zeros(acc.shape, jnp.float32)
    quarter = tile_cols // 4
    for t in range(n_tiles):
        acc[spread(meta_ref[1, t], place, quarter)] += prods[t]
    for i, ref in enumerate((q0, q1, q2, q3)):
        ref[...] = acc[pl.ds(i * quarter, quarter)]


def last_dual_kernel(tile_rows, width, meta_ref, y_ref, demand_ref, sigma_ref, l_ref, l2_ref, r_ref, r2_ref, *rest):
    dual_ref = rest[-1]
    scen = y_ref.shape[0]
    count = meta_ref[2, 0]
    lane = lax.broadcasted_iota(jnp.int32, (scen, width), 1)
    half = tile_rows // 2
    sigma = sigma_ref[...]
    for j in range(tile_rows):
        at = pl.ds(j * width, width)
        live = (lane < count - j * width).astype(jnp.float32)
        if j < half:
            kx = l_ref[j] + l2_ref[j]
        else:
            kx = r_ref[j - half] + r2_ref[j - half]
        dual_ref[:, at] = jnp.maximum(y_ref[:, at] + sigma * (demand_ref[:, at] - kx), 0.0) * live


def primal_kernel(n_tiles, tile_rows, tile_cols, width, has_into, out_at, *refs):
    (meta_ref, tiles_ref, x_ref, cost_ref, upper_ref, tau_ref,
     k0, k1, k2, k3) = refs[:10]
    refs = refs[10 + has_into:]
    if out_at is not None:
        *refs, new_ref, sem = refs
    primal_ref, l_ref, r_ref, extra, prods, acc = refs
    if out_at is not None:
        out_ref, primal_ref = primal_ref, new_ref
    scen = x_ref.shape[0]
    place = meta_ref[2, 1]
    quarter = tile_cols // 4
    half = tile_rows // 2
    tau = tau_ref[...]
    for i, ref in enumerate((k0, k1, k2, k3)):
        base = (place ^ i) * quarter
        for j in range(quarter):
            at = pl.ds(pl.multiple_of((base + j) * width, width), width)
            old = x_ref[:, at]
            new = jnp.minimum(
                jnp.maximum(old - tau * (cost_ref[:, at] - ref[j]), 0.0), upper_ref[:, at]
            )
            primal_ref[:, at] = new
            extra[base + j] = (2.0 * new - old).astype(jnp.bfloat16)
    if out_at is not None:
        out = pltpu.make_async_copy(new_ref, out_ref.at[pl.ds(out_at, scen)], sem)
        out.start()
    for t in range(n_tiles):
        prods[t] = lax.dot_general(
            extra[meta_ref[1, t]], tiles_ref[t], (((1,), (1,)), ((), ())),
            preferred_element_type=jnp.float32,
        )
    acc[...] = jnp.zeros(acc.shape, jnp.float32)
    for t in range(n_tiles):
        acc[meta_ref[0, t]] += prods[t]
    l_ref[...] = acc[pl.ds(0, half)]
    r_ref[...] = acc[pl.ds(half, half)]
    if out_at is not None:
        out.wait()


def body(tiles, tile_row, tile_col, row_count, x_start, y_start, cost, upper, demand, tau, sigma,
         *, n_plant, n_col):
    f32 = jnp.float32
    blocks = tiles[0, 0]
    rows = tile_row[0, 0]
    cols = tile_col[0, 0]
    n_tiles, width, _ = blocks.shape
    scenarios, rows_dev = y_start.shape
    col_width = x_start.shape[1]
    tile_rows = rows_dev // width
    tile_cols = col_width // width
    quarter = tile_cols // 4
    half = tile_rows // 2
    m = scenarios // GROUPS
    plant = lax.axis_index("plant")
    place = ((plant & 1) << 1) | ((plant >> 1) & 1)
    lane = lax.iota(jnp.int32, n_tiles)
    meta = jnp.stack([rows, cols, jnp.where(lane == 0, row_count[0], place)])
    cost_row = cost[None, :]
    upper_row = upper[None, :]
    tau_col = jnp.broadcast_to(tau[:, None], (scenarios, width))
    sigma_col = jnp.broadcast_to(sigma[:, None], (scenarios, width))
    params = pltpu.CompilerParams(vmem_limit_bytes=VMEM_LIMIT)
    quarters = [jax.ShapeDtypeStruct((quarter, m, width), f32)] * 4
    halves = [jax.ShapeDtypeStruct((half, m, width), f32)] * 2
    flops = 2 * n_tiles * m * width * width
    dual_estimate = pl.CostEstimate(flops=DUAL_COST, bytes_accessed=DUAL_COST // 100, transcendentals=0)
    primal_estimate = pl.CostEstimate(flops=PRIMAL_COST, bytes_accessed=PRIMAL_COST // 100, transcendentals=0)

    def swap(value, axis, size, bit):
        return lax.ppermute(value, axis, [(i, i ^ bit) for i in range(size)])

    def y_spec(arr, group):
        return row_block(m, rows_dev, group if arr.shape[0] == scenarios else 0)

    def x_spec(arr, group):
        return row_block(m, col_width, group if arr.shape[0] == scenarios else 0)

    def step_dual(group, dual, parts):
        first = parts is None
        args = [meta, blocks, dual]
        specs = [scalars(), whole(blocks.shape), y_spec(dual, group)]
        if not first:
            args += [demand, sigma_col, *parts]
            specs += [y_spec(demand, group), row_block(m, width, group)] + [whole((half, m, width))] * 4
        return pl.pallas_call(
            functools.partial(dual_kernel, first, n_tiles, tile_rows, tile_cols, width),
            grid=(1,),
            in_specs=specs,
            out_shape=[jax.ShapeDtypeStruct((m, rows_dev), f32)] + quarters,
            out_specs=[whole((m, rows_dev))] + [whole((quarter, m, width))] * 4,
            scratch_shapes=[
                pltpu.VMEM((tile_rows, m, width), jnp.bfloat16),
                pltpu.VMEM((n_tiles, m, width), f32),
                pltpu.VMEM((tile_cols, m, width), f32),
            ],
            compiler_params=params,
            cost_estimate=dual_estimate,
            name="dual_step",
        )(*args)

    def step_primal(group, primal, kty, into, last):
        args = [meta, blocks, primal, cost_row, upper_row, tau_col, *kty]
        specs = [scalars(), whole(blocks.shape), x_spec(primal, group),
                 whole((1, col_width)), whole((1, col_width)), row_block(m, width, group)]
        specs += [whole((quarter, m, width))] * 4
        aliases = {}
        if into is not None:
            aliases = {len(args): 0}
            args.append(into)
            specs.append(pl.BlockSpec(memory_space=pl.ANY))
        out = jax.ShapeDtypeStruct((scenarios if last else m, col_width), f32)
        return pl.pallas_call(
            functools.partial(primal_kernel, n_tiles, tile_rows, tile_cols, width, int(into is not None),
                              group * m if last else None),
            grid=(1,),
            in_specs=specs,
            out_shape=[out] + halves,
            out_specs=[pl.BlockSpec(memory_space=pltpu.HBM) if last else whole((m, col_width))]
            + [whole((half, m, width))] * 2,
            scratch_shapes=[
                pltpu.VMEM((tile_cols, m, width), jnp.bfloat16),
                pltpu.VMEM((n_tiles, m, width), f32),
                pltpu.VMEM((tile_rows, m, width), f32),
            ] + ([pltpu.VMEM((m, col_width), f32), pltpu.SemaphoreType.DMA] if last else []),
            input_output_aliases=aliases,
            compiler_params=params,
            cost_estimate=primal_estimate,
            name="primal_step",
        )(*args)

    def finish_dual(group, dual, parts, into):
        args = [meta, dual, demand, sigma_col, *parts]
        specs = [scalars(), y_spec(dual, group), y_spec(demand, group), row_block(m, width, group)]
        specs += [whole((half, m, width))] * 4
        aliases = {}
        if into is not None:
            aliases = {len(args): 0}
            args.append(into)
            specs.append(pl.BlockSpec(memory_space=pl.ANY))
        return pl.pallas_call(
            functools.partial(last_dual_kernel, tile_rows, width),
            grid=(1,),
            in_specs=specs,
            out_shape=jax.ShapeDtypeStruct((scenarios, rows_dev), f32),
            out_specs=row_block(m, rows_dev, group),
            input_output_aliases=aliases,
            compiler_params=params,
            name="dual_end",
        )(*args)

    final = {"primal": None, "dual": None}

    def run(group):
        dual, primal, parts = y_start, x_start, None
        for iteration in range(ITERS):
            last = iteration == ITERS - 1
            dual, q0, q1, q2, q3 = step_dual(group, dual, parts)
            g1 = swap(q3, "plant", n_plant, 1)
            g0 = swap(q2, "plant", n_plant, 1)
            q1, g1 = yield q1, g1
            q1 = swap(q1 + g1, "plant", n_plant, 2)
            q0, g0, q1 = yield q0, g0, q1
            own = q0 + g0 + q1
            bit = 4
            while bit < n_plant:
                near = swap(own, "plant", n_plant, bit)
                bit *= 2
                own, near = yield own, near
                own = own + near
            pair = swap(own, "plant", n_plant, 2)
            other = swap(own, "plant", n_plant, 1)
            own, pair = yield own, pair
            across = swap(pair, "plant", n_plant, 1)
            own, pair, other, across = yield own, pair, other, across
            kty = (own, pair, other, across)
            into = final["primal"] if last else None
            primal, l, r = step_primal(group, primal, kty, into, last)
            if last:
                final["primal"] = primal
            for a, b in zip(bits, turned):
                l2, r2 = swap(l, "col", n_col, a), swap(r, "col", n_col, b)
                l, l2, r, r2 = yield l, l2, r, r2
                if a != bits[-1]:
                    l, r = l + l2, r + r2
            parts = (l, l2, r, r2)
        final["dual"] = finish_dual(group, dual, parts, final["dual"])

    bits = []
    bit = 1
    while bit < n_col:
        bits.append(bit)
        bit *= 2
    turned = bits[len(bits) // 2:] + bits[:len(bits) // 2]
    runs = [run(g) for g in range(GROUPS)]
    held = [next(r) for r in runs]
    token = None
    for g in order(GROUPS, n_plant, n_col):
        values = held[g]
        if TIE:
            if token is not None:
                *values, token = lax.optimization_barrier((*values, token))
            else:
                token = values[0]
                values = list(values)
        try:
            held[g] = runs[g].send(tuple(values))
            if TIE:
                token, _ = lax.optimization_barrier((token, held[g][0]))
        except StopIteration:
            pass
    return final["primal"], final["dual"]


def order(groups, n_plant, n_col):
    mids = max(n_plant.bit_length() - 3, 0)
    lengths = STEPS[:2] + STEPS[2:3] * mids + STEPS[3:5] + STEPS[5:6] * (n_col.bit_length() - 2) + STEPS[6:]
    events = []
    for g in range(groups):
        at = LAG * g
        for i in range(ITERS):
            for j, length in enumerate(lengths):
                at += length
                events.append((at, g))
    return [g for _, g in sorted(events)]


def solution(mesh):
    placed = (
        P("plant", "col", None, None, None),
        P("plant", "col", None),
        P("plant", "col", None),
        P("plant"),
        P(None, "col"),
        P(None, "plant"),
        P("col"),
        P("col"),
        P(None, "plant"),
        P(),
        P(),
    )
    return jax.shard_map(
        functools.partial(body, n_plant=mesh.shape["plant"], n_col=mesh.shape["col"]),
        mesh=mesh,
        in_specs=placed,
        out_specs=(P(None, "col"), P(None, "plant")),
        check_vma=False,
    )
```

```python
import functools

import jax
import jax.numpy as jnp
from jax import lax
from jax.experimental import pallas as pl
from jax.experimental.pallas import tpu as pltpu
from jax.sharding import PartitionSpec as P

ITERS = 3
GROUPS = 2
VMEM_LIMIT = 24 << 20
LAG = 19.4
STEPS = [4.0, 11.1, 15.0, 8.9, 2.0, 8.0, 8.4]
DUAL_COST = 10**11
PRIMAL_COST = 10**11
TIE = True


def row_block(rows, width, group):
    return pl.BlockSpec((rows, width), lambda i: (group, 0))


def whole(shape):
    return pl.BlockSpec(shape, lambda i: (0,) * len(shape))


def scalars():
    return pl.BlockSpec(memory_space=pltpu.SMEM)


def spread(col, place, quarter):
    if quarter & (quarter - 1):
        part = lax.div(col, quarter)
        return (part ^ place) * quarter + (col - part * quarter)
    return col ^ (place * quarter)


def dual_kernel(first, y_at, n_tiles, tile_rows, tile_cols, width, *refs):
    if first:
        *refs, y_buf, sem = refs
        (meta_ref, tiles_ref, y_ref,
         dual_ref, q0, q1, q2, q3, low, prods, acc) = refs
    else:
        (meta_ref, tiles_ref, y_ref, demand_ref, sigma_ref,
         l_ref, l2_ref, r_ref, r2_ref,
         dual_ref, q0, q1, q2, q3, low, prods, acc) = refs
    if first:
        copy = pltpu.make_async_copy(y_ref.at[pl.ds(y_at, y_buf.shape[0])], y_buf, sem)
        copy.start()
        copy.wait()
        y_ref = y_buf
    scen = y_ref.shape[0]
    count, place = meta_ref[2, 0], meta_ref[2, 1]
    lane = lax.broadcasted_iota(jnp.int32, (scen, width), 1)
    half = tile_rows // 2
    if not first:
        sigma = sigma_ref[...]
    for j in range(tile_rows):
        at = pl.ds(j * width, width)
        live = (lane < count - j * width).astype(jnp.float32)
        if first:
            dual = y_ref[:, at] * live
        else:
            if j < half:
                kx = l_ref[j] + l2_ref[j]
            else:
                kx = r_ref[j - half] + r2_ref[j - half]
            dual = jnp.maximum(y_ref[:, at] + sigma * (demand_ref[:, at] - kx), 0.0) * live
        dual_ref[:, at] = dual
        low[j] = dual.astype(jnp.bfloat16)
    for t in range(n_tiles):
        prods[t] = jnp.dot(low[meta_ref[0, t]], tiles_ref[t], preferred_element_type=jnp.float32)
    acc[...] = jnp.zeros(acc.shape, jnp.float32)
    quarter = tile_cols // 4
    for t in range(n_tiles):
        acc[spread(meta_ref[1, t], place, quarter)] += prods[t]
    for i, ref in enumerate((q0, q1, q2, q3)):
        ref[...] = acc[pl.ds(i * quarter, quarter)]


def last_dual_kernel(tile_rows, width, meta_ref, y_ref, demand_ref, sigma_ref, l_ref, l2_ref, r_ref, r2_ref, *rest):
    dual_ref = rest[-1]
    scen = y_ref.shape[0]
    count = meta_ref[2, 0]
    lane = lax.broadcasted_iota(jnp.int32, (scen, width), 1)
    half = tile_rows // 2
    sigma = sigma_ref[...]
    for j in range(tile_rows):
        at = pl.ds(j * width, width)
        live = (lane < count - j * width).astype(jnp.float32)
        if j < half:
            kx = l_ref[j] + l2_ref[j]
        else:
            kx = r_ref[j - half] + r2_ref[j - half]
        dual_ref[:, at] = jnp.maximum(y_ref[:, at] + sigma * (demand_ref[:, at] - kx), 0.0) * live


def primal_kernel(n_tiles, tile_rows, tile_cols, width, has_into, out_at, *refs):
    (meta_ref, tiles_ref, x_ref, cost_ref, upper_ref, tau_ref,
     k0, k1, k2, k3) = refs[:10]
    refs = refs[10 + has_into:]
    if out_at is not None:
        *refs, new_ref, sem = refs
    primal_ref, l_ref, r_ref, extra, prods, acc = refs
    if out_at is not None:
        out_ref, primal_ref = primal_ref, new_ref
    scen = x_ref.shape[0]
    place = meta_ref[2, 1]
    quarter = tile_cols // 4
    half = tile_rows // 2
    tau = tau_ref[...]
    for i, ref in enumerate((k0, k1, k2, k3)):
        base = (place ^ i) * quarter
        for j in range(quarter):
            at = pl.ds(pl.multiple_of((base + j) * width, width), width)
            old = x_ref[:, at]
            new = jnp.minimum(
                jnp.maximum(old - tau * (cost_ref[:, at] - ref[j]), 0.0), upper_ref[:, at]
            )
            primal_ref[:, at] = new
            extra[base + j] = (2.0 * new - old).astype(jnp.bfloat16)
    if out_at is not None:
        out = pltpu.make_async_copy(new_ref, out_ref.at[pl.ds(out_at, scen)], sem)
        out.start()
    for t in range(n_tiles):
        prods[t] = lax.dot_general(
            extra[meta_ref[1, t]], tiles_ref[t], (((1,), (1,)), ((), ())),
            preferred_element_type=jnp.float32,
        )
    acc[...] = jnp.zeros(acc.shape, jnp.float32)
    for t in range(n_tiles):
        acc[meta_ref[0, t]] += prods[t]
    l_ref[...] = acc[pl.ds(0, half)]
    r_ref[...] = acc[pl.ds(half, half)]
    if out_at is not None:
        out.wait()


def body(tiles, tile_row, tile_col, row_count, x_start, y_start, cost, upper, demand, tau, sigma,
         *, n_plant, n_col):
    f32 = jnp.float32
    blocks = tiles[0, 0]
    rows = tile_row[0, 0]
    cols = tile_col[0, 0]
    n_tiles, width, _ = blocks.shape
    scenarios, rows_dev = y_start.shape
    col_width = x_start.shape[1]
    tile_rows = rows_dev // width
    tile_cols = col_width // width
    quarter = tile_cols // 4
    half = tile_rows // 2
    m = scenarios // GROUPS
    plant = lax.axis_index("plant")
    place = ((plant & 1) << 1) | ((plant >> 1) & 1)
    lane = lax.iota(jnp.int32, n_tiles)
    meta = jnp.stack([rows, cols, jnp.where(lane == 0, row_count[0], place)])
    cost_row = cost[None, :]
    upper_row = upper[None, :]
    tau_col = jnp.broadcast_to(tau[:, None], (scenarios, width))
    sigma_col = jnp.broadcast_to(sigma[:, None], (scenarios, width))
    params = pltpu.CompilerParams(vmem_limit_bytes=VMEM_LIMIT)
    quarters = [jax.ShapeDtypeStruct((quarter, m, width), f32)] * 4
    halves = [jax.ShapeDtypeStruct((half, m, width), f32)] * 2
    flops = 2 * n_tiles * m * width * width
    dual_estimate = pl.CostEstimate(flops=DUAL_COST, bytes_accessed=DUAL_COST // 100, transcendentals=0)
    primal_estimate = pl.CostEstimate(flops=PRIMAL_COST, bytes_accessed=PRIMAL_COST // 100, transcendentals=0)

    def swap(value, axis, size, bit):
        return lax.ppermute(value, axis, [(i, i ^ bit) for i in range(size)])

    def y_spec(arr, group):
        return row_block(m, rows_dev, group if arr.shape[0] == scenarios else 0)

    def x_spec(arr, group):
        return row_block(m, col_width, group if arr.shape[0] == scenarios else 0)

    def step_dual(group, dual, parts):
        first = parts is None
        args = [meta, blocks, dual]
        specs = [scalars(), whole(blocks.shape), y_spec(dual, group)]
        if first:
            specs[2] = pl.BlockSpec(memory_space=pltpu.HBM)
        else:
            args += [demand, sigma_col, *parts]
            specs += [y_spec(demand, group), row_block(m, width, group)] + [whole((half, m, width))] * 4
        return pl.pallas_call(
            functools.partial(dual_kernel, first, group * m, n_tiles, tile_rows, tile_cols, width),
            grid=(1,),
            in_specs=specs,
            out_shape=[jax.ShapeDtypeStruct((m, rows_dev), f32)] + quarters,
            out_specs=[whole((m, rows_dev))] + [whole((quarter, m, width))] * 4,
            scratch_shapes=[
                pltpu.VMEM((tile_rows, m, width), jnp.bfloat16),
                pltpu.VMEM((n_tiles, m, width), f32),
                pltpu.VMEM((tile_cols, m, width), f32),
            ] + ([pltpu.VMEM((m, rows_dev), f32), pltpu.SemaphoreType.DMA] if first else []),
            compiler_params=params,
            cost_estimate=dual_estimate,
            name="dual_step",
        )(*args)

    def step_primal(group, primal, kty, into, last):
        args = [meta, blocks, primal, cost_row, upper_row, tau_col, *kty]
        specs = [scalars(), whole(blocks.shape), x_spec(primal, group),
                 whole((1, col_width)), whole((1, col_width)), row_block(m, width, group)]
        specs += [whole((quarter, m, width))] * 4
        aliases = {}
        if into is not None:
            aliases = {len(args): 0}
            args.append(into)
            specs.append(pl.BlockSpec(memory_space=pl.ANY))
        out = jax.ShapeDtypeStruct((scenarios if last else m, col_width), f32)
        return pl.pallas_call(
            functools.partial(primal_kernel, n_tiles, tile_rows, tile_cols, width, int(into is not None),
                              group * m if last else None),
            grid=(1,),
            in_specs=specs,
            out_shape=[out] + halves,
            out_specs=[pl.BlockSpec(memory_space=pltpu.HBM) if last else whole((m, col_width))]
            + [whole((half, m, width))] * 2,
            scratch_shapes=[
                pltpu.VMEM((tile_cols, m, width), jnp.bfloat16),
                pltpu.VMEM((n_tiles, m, width), f32),
                pltpu.VMEM((tile_rows, m, width), f32),
            ] + ([pltpu.VMEM((m, col_width), f32), pltpu.SemaphoreType.DMA] if last else []),
            input_output_aliases=aliases,
            compiler_params=params,
            cost_estimate=primal_estimate,
            name="primal_step",
        )(*args)

    def finish_dual(group, dual, parts, into):
        args = [meta, dual, demand, sigma_col, *parts]
        specs = [scalars(), y_spec(dual, group), y_spec(demand, group), row_block(m, width, group)]
        specs += [whole((half, m, width))] * 4
        aliases = {}
        if into is not None:
            aliases = {len(args): 0}
            args.append(into)
            specs.append(pl.BlockSpec(memory_space=pl.ANY))
        return pl.pallas_call(
            functools.partial(last_dual_kernel, tile_rows, width),
            grid=(1,),
            in_specs=specs,
            out_shape=jax.ShapeDtypeStruct((scenarios, rows_dev), f32),
            out_specs=row_block(m, rows_dev, group),
            input_output_aliases=aliases,
            compiler_params=params,
            name="dual_end",
        )(*args)

    final = {"primal": None, "dual": None}

    def run(group):
        dual, primal, parts = y_start, x_start, None
        for iteration in range(ITERS):
            last = iteration == ITERS - 1
            dual, q0, q1, q2, q3 = step_dual(group, dual, parts)
            g1 = swap(q3, "plant", n_plant, 1)
            g0 = swap(q2, "plant", n_plant, 1)
            q1, g1 = yield q1, g1
            q1 = swap(q1 + g1, "plant", n_plant, 2)
            q0, g0, q1 = yield q0, g0, q1
            own = q0 + g0 + q1
            bit = 4
            while bit < n_plant:
                near = swap(own, "plant", n_plant, bit)
                bit *= 2
                own, near = yield own, near
                own = own + near
            pair = swap(own, "plant", n_plant, 2)
            other = swap(own, "plant", n_plant, 1)
            own, pair = yield own, pair
            across = swap(pair, "plant", n_plant, 1)
            own, pair, other, across = yield own, pair, other, across
            kty = (own, pair, other, across)
            into = final["primal"] if last else None
            primal, l, r = step_primal(group, primal, kty, into, last)
            if last:
                final["primal"] = primal
            for a, b in zip(bits, turned):
                l2, r2 = swap(l, "col", n_col, a), swap(r, "col", n_col, b)
                l, l2, r, r2 = yield l, l2, r, r2
                if a != bits[-1]:
                    l, r = l + l2, r + r2
            parts = (l, l2, r, r2)
        final["dual"] = finish_dual(group, dual, parts, final["dual"])

    bits = []
    bit = 1
    while bit < n_col:
        bits.append(bit)
        bit *= 2
    turned = bits[len(bits) // 2:] + bits[:len(bits) // 2]
    runs = [run(g) for g in range(GROUPS)]
    held = [next(r) for r in runs]
    token = None
    for g in order(GROUPS, n_plant, n_col):
        values = held[g]
        if TIE:
            if token is not None:
                *values, token = lax.optimization_barrier((*values, token))
            else:
                token = values[0]
                values = list(values)
        try:
            held[g] = runs[g].send(tuple(values))
            if TIE:
                token, _ = lax.optimization_barrier((token, held[g][0]))
        except StopIteration:
            pass
    return final["primal"], final["dual"]


def order(groups, n_plant, n_col):
    mids = max(n_plant.bit_length() - 3, 0)
    lengths = STEPS[:2] + STEPS[2:3] * mids + STEPS[3:5] + STEPS[5:6] * (n_col.bit_length() - 2) + STEPS[6:]
    events = []
    for g in range(groups):
        at = LAG * g
        for i in range(ITERS):
            for j, length in enumerate(lengths):
                at += length
                events.append((at, g))
    return [g for _, g in sorted(events)]


def solution(mesh):
    placed = (
        P("plant", "col", None, None, None),
        P("plant", "col", None),
        P("plant", "col", None),
        P("plant"),
        P(None, "col"),
        P(None, "plant"),
        P("col"),
        P("col"),
        P(None, "plant"),
        P(),
        P(),
    )
    return jax.shard_map(
        functools.partial(body, n_plant=mesh.shape["plant"], n_col=mesh.shape["col"]),
        mesh=mesh,
        in_specs=placed,
        out_specs=(P(None, "col"), P(None, "plant")),
        check_vma=False,
    )
```
